32 devices in a mesh: rep: 4 (over y, x), fsdp: 8 (over z, core).
Axes of the slice: x: 2, y: 2, z: 4, core: 2. Of those that a mesh axis runs over, the one named last changes fastest.
Arguments:
- tokens: bfloat16 [8192, 1280], P(('rep', 'fsdp')), may hold values from -6 to 6
- cotangent: bfloat16 [8192, 1280], P(('rep', 'fsdp')), may hold values from -6 to 6
- lengths: int32 [16], replicated, may hold values from 1 to 1024, 8192 in all
- sequence_order: int32 [16], replicated, may hold values from 0 to 15, each once
- expert_choice: int32 [8192, 7], P(('rep', 'fsdp')), may hold values from 0 to 15, all different within a row; in each aligned block of 256 rows (0 to 255, 256 to 511, ...) at most 224 rows name the same one
- expert_home: int32 [16], replicated, may hold values from 0 to 15, each once
- first_gain: bfloat16 [1280], P('fsdp'), may hold values from 0.5 to 1.5
- w_query: bfloat16 [1280, 1280], P('fsdp'), may hold values from -0.15625 to 0.15625
- w_key: bfloat16 [1280, 1280], P('fsdp'), may hold values from -0.15625 to 0.15625
- w_value: bfloat16 [1280, 1280], P('fsdp'), may hold values from -0.15625 to 0.15625
- w_out: bfloat16 [1280, 1280], P('fsdp'), may hold values from -1 to 1
- second_gain: bfloat16 [1280], P('fsdp'), may hold values from 0.5 to 1.5
- w_router: bfloat16 [1280, 16], P('fsdp'), may hold values from -0.083984375 to 0.083984375
- shared_gate: bfloat16 [1280, 896], P('fsdp'), may hold values from -0.15625 to 0.15625
- shared_up: bfloat16 [1280, 896], P('fsdp'), may hold values from -0.15625 to 0.15625
- shared_down: bfloat16 [896, 1280], P('fsdp'), may hold values from -0.25 to 0.25
- expert_gate: bfloat16 [16, 1280, 896], P('fsdp'), may hold values from -0.15625 to 0.15625
- expert_up: bfloat16 [16, 1280, 896], P('fsdp'), may hold values from -0.15625 to 0.15625
- expert_down: bfloat16 [16, 896, 1280], P('fsdp'), may hold values from -0.75 to 0.75
Outputs:
- output: bfloat16 [8192, 1280], P(('rep', 'fsdp'))
- input_grad: bfloat16 [8192, 1280], P(('rep', 'fsdp'))
- first_gain_grad: float32 [1280], P('fsdp')
- w_query_grad: float32 [1280, 1280], P('fsdp')
- w_key_grad: float32 [1280, 1280], P('fsdp')
- w_value_grad: float32 [1280, 1280], P('fsdp')
- w_out_grad: float32 [1280, 1280], P('fsdp')
- second_gain_grad: float32 [1280], P('fsdp')
- w_router_grad: float32 [1280, 16], P('fsdp')
- shared_gate_grad: float32 [1280, 896], P('fsdp')
- shared_up_grad: float32 [1280, 896], P('fsdp')
- shared_down_grad: float32 [896, 1280], P('fsdp')
- expert_gate_grad: float32 [16, 1280, 896], P('fsdp')
- expert_up_grad: float32 [16, 1280, 896], P('fsdp')
- expert_down_grad: float32 [16, 896, 1280], P('fsdp')
The draws below stay inside these ranges and needn't reach their ends.
Inputs may be any that keep to these rules, and one draw needn't show every extreme that they name: The lengths add up to 8192, and the longest is exactly 1024. `sequence_order`: a permutation of the 16 sequences. `expert_choice`: each token names 7 different experts; of the 256 tokens of one device at most 224 name any one expert, and on some device some expert is named by exactly 224 of them. `expert_home`: a permutation of the 16 weight slots.
All inputs are finite; a program needn't handle non-finite values.
Results may differ from the reference program's by a relative error of at most 0.023.
Values may be sent and summed in bfloat16 or wider, within the bound.
A program may use at most 320 MiB of HBM per device.

```python
import math
from functools import partial
import jax
import jax.numpy as jnp
import numpy as np
from jax import lax

MODEL_WIDTH = 1280
HEADS = 10
DH = 128
FF = 896
TOP = 7
TOK_DEV = 256
SEQ_MAX = 1024
TOTAL_TOKENS = 8192
SEQS = 16
ROUTED_EXPERTS = 16
CAP = 224
DEVICES = 32


def block_levels(own_key, extent, pieces, low, largest):
    def one(dim, shards_of):
        draws = jax.random.uniform(jax.random.fold_in(jax.random.fold_in(own_key, 6), dim), (shards_of,), jnp.float32, low / len(pieces), largest / len(pieces))
        return jnp.repeat(jnp.exp(draws), extent[dim] // shards_of).reshape((-1,) + (1,) * (len(extent) - dim - 1))

    gain = one(*pieces[0])
    for cut in pieces[1:]:
        gain = gain * one(*cut)
    return gain


def profile(amount, total, limit, skew):
    portions = [(1 << 20) // math.isqrt(rank ** skew) + 1 for rank in range(2, amount + 1)]
    rest, counts = total - limit - (amount - 1), [1] * (amount - 1)
    while rest > 0:
        movable = [i for i in range(amount - 1) if counts[i] < limit]
        whole, left = sum([portions[i] for i in movable]), rest
        for i in movable:
            addition = min(limit - counts[i], max(1, left * portions[i] // whole), rest)
            counts[i] = counts[i] + addition
            rest = rest - addition
    return np.array([limit] + counts)


def ragged_sizes(key, amount, total, bound, skew):
    if amount == 2:
        one = jax.random.randint(key, (), max(1, total - bound), min(bound, total - 1) + 1)
        return jnp.stack([one, total - one])
    sizes = jnp.asarray(profile(amount, total, bound, skew), jnp.int32)
    couples = (amount - 1) // 2
    donor, taker = sizes[1:1 + 2 * couples:2], sizes[2:2 + 2 * couples:2]
    slack = jnp.minimum(donor - 1, bound - taker)
    moved = jax.random.randint(jax.random.fold_in(key, 1), (couples,), 0, 1 << 20) % (slack + 1)
    sizes = sizes.at[1:1 + 2 * couples:2].set(donor - moved).at[2:2 + 2 * couples:2].set(taker + moved)
    return sizes[jax.random.permutation(jax.random.fold_in(key, 2), amount)]


def routed_block(stream_key, own, number, rows, number_of, top, bound, skew):
    sequence = jax.random.permutation(stream_key, number_of)
    heavy_load, usual = load_shares(number_of, rows * top, bound, skew, True), load_shares(number_of, rows * top, bound, skew, False)
    places = jnp.arange(number_of)

    def named(tallies, turn):
        used = int((tallies > 0).sum())
        fixed = max(1, used // 4)
        moved = fixed + (places - fixed + turn * (used - fixed)) % max(1, number_of - fixed)
        return jnp.zeros((number_of,), jnp.int32).at[sequence[jnp.where(places < fixed, places, moved)]].set(jnp.asarray(tallies, jnp.int32))

    tallies = jnp.where(number % 4 == 0, named(heavy_load, number // 4), named(usual, number - number // 4 - 1))
    mixed = jax.random.permutation(jax.random.fold_in(own, 3), number_of)
    donor, sink = mixed[0:number_of // 2 * 2:2], mixed[1:number_of // 2 * 2:2]
    slack = jnp.minimum(tallies[donor] - 1, bound - tallies[sink]) // 2
    slack = jnp.where((donor == sequence[0]) | (sink == sequence[0]) | (tallies[sink] == 0), 0, jnp.maximum(slack, 0))
    moved = jax.random.randint(jax.random.fold_in(own, 4), (number_of // 2,), 0, 1 << 20) % (slack + 1)
    tallies = tallies.at[donor].add(-moved).at[sink].add(moved)
    members = jnp.searchsorted(jnp.cumsum(tallies), jnp.arange(rows * top), side="right").astype(jnp.int32)
    listing = members.reshape(top, rows).T
    listing = listing[jax.random.permutation(jax.random.fold_in(own, 1), rows)]
    turn = jax.random.randint(jax.random.fold_in(own, 2), (rows, 1), 0, top)
    return jnp.take_along_axis(listing, (jnp.arange(top)[None, :] + turn) % top, axis=1)


def load_shares(number_of, total, bound, skew, full):
    weights = [(1 << 20) // math.isqrt(grade ** skew) + 1 for grade in range(1, number_of + 1)]
    largest = bound if full else min(bound, max(-(-total // number_of), total * weights[0] // sum(weights)))
    least = 1 if total - largest >= number_of - 1 else 0
    counts, rest = [largest] + [least] * (number_of - 1), total - largest - least * (number_of - 1)
    while rest > 0:
        movable = [i for i in range(1, number_of) if counts[i] < largest] or [i for i in range(1, number_of) if counts[i] < bound]
        mass, budget = sum([weights[i] for i in movable]), rest
        for i in movable:
            extra = min(bound - counts[i], max(1, budget * weights[i] // mass), rest)
            counts[i] = counts[i] + extra
            rest = rest - extra
    return np.array(counts)


def gaussian(own_key, shape, width, bound, shards=(), kind=jnp.bfloat16):
    loudness = block_levels(own_key, shape, shards, -0.22, 0.18) if shards else 1.0
    values = jax.random.normal(own_key, shape, jnp.float32) * width * loudness
    return jnp.minimum(jnp.maximum(values, -bound), bound).astype(kind)


def setup_inputs(seed: int = 0) -> dict:
    seeds = jax.random.split(jax.random.key(seed), 20)
    tokens = gaussian(seeds[0], (TOTAL_TOKENS, MODEL_WIDTH), 1.0, 6.0, ((0, 32),))
    cotangent = gaussian(seeds[1], (TOTAL_TOKENS, MODEL_WIDTH), 1.0, 6.0, ((0, 32),))
    lengths = ragged_sizes(seeds[2], SEQS, TOTAL_TOKENS, SEQ_MAX, 1).astype(jnp.int32)
    sequence_order = jax.random.permutation(seeds[3], SEQS).astype(jnp.int32)
    expert_choice_keys = jax.random.split(jax.random.fold_in(seeds[4], 1), TOTAL_TOKENS // TOK_DEV)
    expert_choice_turns = jax.random.permutation(jax.random.fold_in(seeds[4], 3), TOTAL_TOKENS // TOK_DEV)
    expert_choice = jax.vmap(lambda own, number: routed_block(jax.random.fold_in(seeds[4], 2), own, number, TOK_DEV, ROUTED_EXPERTS, TOP, CAP, 1))(expert_choice_keys, expert_choice_turns).reshape((TOTAL_TOKENS, TOP))
    expert_home = jax.random.permutation(seeds[5], ROUTED_EXPERTS).astype(jnp.int32)
    first_gain = jnp.clip(1.0 + 0.1 * jax.random.normal(seeds[6], (MODEL_WIDTH,), jnp.float32), 0.5, 1.5).astype(jnp.bfloat16)
    w_query = gaussian(seeds[7], (MODEL_WIDTH, HEADS * DH), MODEL_WIDTH ** -0.5, 0.15625, ((0, 8),))
    w_key = gaussian(seeds[8], (MODEL_WIDTH, HEADS * DH), MODEL_WIDTH ** -0.5, 0.15625, ((0, 8),))
    w_value = gaussian(seeds[9], (MODEL_WIDTH, HEADS * DH), MODEL_WIDTH ** -0.5, 0.15625, ((0, 8),))
    w_out = gaussian(seeds[10], (HEADS * DH, MODEL_WIDTH), (HEADS * DH // 32) ** -0.5, 1.0, ((0, 8),))
    second_gain = jnp.clip(1.0 + 0.1 * jax.random.normal(seeds[11], (MODEL_WIDTH,), jnp.float32), 0.5, 1.5).astype(jnp.bfloat16)
    w_router = gaussian(seeds[12], (MODEL_WIDTH, ROUTED_EXPERTS), 0.014, 0.083984375, ((0, 8),))
    shared_gate = gaussian(seeds[13], (MODEL_WIDTH, FF), MODEL_WIDTH ** -0.5, 0.15625, ((0, 8),))
    shared_up = gaussian(seeds[14], (MODEL_WIDTH, FF), MODEL_WIDTH ** -0.5, 0.15625, ((0, 8),))
    shared_down = gaussian(seeds[15], (FF, MODEL_WIDTH), (FF // 2) ** -0.5, 0.25, ((0, 8),))
    expert_gate = gaussian(seeds[16], (ROUTED_EXPERTS, MODEL_WIDTH, FF), MODEL_WIDTH ** -0.5, 0.15625, ((0, 8),))
    expert_up = gaussian(seeds[17], (ROUTED_EXPERTS, MODEL_WIDTH, FF), MODEL_WIDTH ** -0.5, 0.15625, ((0, 8),))
    expert_down = gaussian(seeds[18], (ROUTED_EXPERTS, FF, MODEL_WIDTH), (FF // 16) ** -0.5, 0.75, ((0, 8),))
    return {"tokens": tokens, "cotangent": cotangent, "lengths": lengths, "sequence_order": sequence_order, "expert_choice": expert_choice, "expert_home": expert_home, "first_gain": first_gain, "w_query": w_query, "w_key": w_key, "w_value": w_value, "w_out": w_out, "second_gain": second_gain, "w_router": w_router, "shared_gate": shared_gate, "shared_up": shared_up, "shared_down": shared_down, "expert_gate": expert_gate, "expert_up": expert_up, "expert_down": expert_down}


EPSILON = 1e-06
NEGATIVE = -1e+30
HIGHEST = lax.Precision.HIGHEST

@jax.custom_vjp
def low(v):
    return lax.optimization_barrier(v.astype(jnp.bfloat16)).astype(jnp.float32)

@jax.custom_vjp
def low_back(v):
    return v

def low_keep(v):
    return (low(v), None)

def low_pass(kept, grad):
    return (grad,)

def back_keep(v):
    return (v, None)

def back_low(kept, grad):
    return (low(grad),)
low.defvjp(low_keep, low_pass)
low_back.defvjp(back_keep, back_low)

def matmul(left, right):
    return jnp.dot(left, right, precision=HIGHEST, preferred_element_type=jnp.float32)

def rms_scale(values):
    return lax.rsqrt(lax.optimization_barrier(jnp.mean(values * values, axis=1, keepdims=True)) + EPSILON)

def silu_value(values):
    return values / (1.0 + jnp.exp(-values))

def rotary_tables(position, head_size):
    half_size = head_size // 2
    frequency = 1.0 / 10000.0 ** (jnp.arange(half_size, dtype=jnp.float32) / half_size)
    angles = position.astype(jnp.float32)[:, None] * frequency[None, :]
    cosine_table = jnp.cos(angles)
    sine_table = jnp.sin(angles)
    cosine_table = jnp.concatenate([cosine_table, cosine_table], axis=1)[:, None, :]
    sine_table = jnp.concatenate([sine_table, sine_table], axis=1)[:, None, :]
    return (cosine_table, sine_table)

def rotate(values, cosine_table, sine_table):
    half_size = values.shape[-1] // 2
    turned = jnp.concatenate([-values[..., half_size:], values[..., :half_size]], axis=-1)
    return values * cosine_table + turned * sine_table

def sequence_starts(lengths, sequence_order, token_index):
    ordered = lengths[sequence_order]
    opening = (jnp.cumsum(ordered) - ordered).astype(jnp.int32)
    chosen_open = jnp.where(opening[None, :] <= token_index[:, None], opening[None, :], 0)
    return lax.optimization_barrier(jnp.max(chosen_open, axis=1)).astype(jnp.int32)

def masked_softmax(scores, visible):
    masked = jnp.where(visible, scores, NEGATIVE)
    top_score = lax.optimization_barrier(jnp.max(masked, axis=-1, keepdims=True))
    expanded = jnp.exp(masked - top_score)
    return expanded / lax.optimization_barrier(jnp.sum(expanded, axis=-1, keepdims=True))

def attention_rows(query_rot, key_padded, value_padded, seq_start, block_index):
    first_row = block_index * TOK_DEV
    queries = lax.dynamic_slice_in_dim(query_rot, first_row, TOK_DEV, 0)
    key_block = lax.dynamic_slice_in_dim(key_padded, first_row, TOK_DEV + SEQ_MAX, 0)
    value_block = lax.dynamic_slice_in_dim(value_padded, first_row, TOK_DEV + SEQ_MAX, 0)
    starts = lax.dynamic_slice_in_dim(seq_start, first_row, TOK_DEV, 0)
    query_index = first_row + jnp.arange(TOK_DEV, dtype=jnp.int32)
    key_index = first_row - SEQ_MAX + jnp.arange(TOK_DEV + SEQ_MAX, dtype=jnp.int32)
    visible = (key_index[None, :] <= query_index[:, None]) & (key_index[None, :] >= starts[:, None])
    scores = low_back(jnp.einsum('qhd,khd->hqk', queries, key_block, precision=HIGHEST) * (1.0 / math.sqrt(DH)))
    weights_soft = masked_softmax(scores, visible[None, :, :])
    return jnp.einsum('hqk,khd->qhd', low(weights_soft), value_block, precision=HIGHEST)

def routed_term(hidden_two, gate_flat, order_padded, slot_counts, slot_open, slot_items):
    slot_index, weight_gate, weight_up, weight_down = slot_items
    span = DEVICES * CAP
    picked = lax.dynamic_slice_in_dim(order_padded, slot_open[slot_index], span, 0)
    live_rows = jnp.arange(span, dtype=jnp.int32) < slot_counts[slot_index]
    token_of = picked // TOP
    row_values = low_back(hidden_two[token_of])
    pre_gate = low_back(matmul(row_values, weight_gate))
    pre_up = low_back(matmul(row_values, weight_up))
    hidden_rows = low(silu_value(pre_gate) * pre_up)
    out_rows = low_back(low(matmul(hidden_rows, weight_down)))
    weight_rows = jnp.where(live_rows, gate_flat[picked], 0.0)
    return jnp.zeros((TOTAL_TOKENS, MODEL_WIDTH), jnp.float32).at[token_of].add(weight_rows[:, None] * out_rows)

def reference(tokens, cotangent, lengths, sequence_order, expert_choice, expert_home, first_gain, w_query, w_key, w_value, w_out, second_gain, w_router, shared_gate, shared_up, shared_down, expert_gate, expert_up, expert_down):
    token_index = jnp.arange(TOTAL_TOKENS, dtype=jnp.int32)
    seq_start = sequence_starts(lengths, sequence_order, token_index)
    cosine_table, sine_table = rotary_tables(token_index - seq_start, DH)
    choice_flat = expert_choice.reshape(-1)
    row_count = choice_flat.shape[0]
    slot_flat = expert_home[choice_flat]
    order_rows = jnp.argsort(slot_flat * row_count + jnp.arange(row_count, dtype=jnp.int32)).astype(jnp.int32)
    slot_hit = (slot_flat[:, None] == jnp.arange(ROUTED_EXPERTS, dtype=jnp.int32)[None, :]).astype(jnp.int32)
    slot_counts = lax.optimization_barrier(jnp.sum(slot_hit, axis=0)).astype(jnp.int32)
    slot_open = (jnp.cumsum(slot_counts) - slot_counts).astype(jnp.int32)
    order_padded = jnp.concatenate([order_rows, jnp.zeros((DEVICES * CAP,), jnp.int32)])
    key_zeros = jnp.zeros((SEQ_MAX, HEADS, DH), jnp.float32)

    def decoder_layer(layer_input, attention_norm_gain, query_matrix, key_matrix, value_matrix, output_matrix, feedforward_norm_gain, router_matrix, common_gate_weight, common_up_weight, common_down_weight, routed_gate_weight, routed_up_weight, routed_down_weight):
        hidden_one = low(layer_input * rms_scale(layer_input) * attention_norm_gain[None, :])
        query_raw = low_back(matmul(hidden_one, query_matrix)).reshape(TOTAL_TOKENS, HEADS, DH)
        key_raw = low_back(matmul(hidden_one, key_matrix)).reshape(TOTAL_TOKENS, HEADS, DH)
        value_low = low(low_back(matmul(hidden_one, value_matrix))).reshape(TOTAL_TOKENS, HEADS, DH)
        query_rot = low(rotate(query_raw, cosine_table, sine_table))
        key_rot = low(rotate(key_raw, cosine_table, sine_table))
        key_padded = jnp.concatenate([key_zeros, key_rot], axis=0)
        value_padded = jnp.concatenate([key_zeros, value_low], axis=0)
        attend = jax.checkpoint(partial(attention_rows, query_rot, key_padded, value_padded, seq_start))
        mixed_rows = lax.map(attend, jnp.arange(DEVICES, dtype=jnp.int32)).reshape(TOTAL_TOKENS, HEADS * DH)
        attended = low_back(low(mixed_rows))
        resid_one = layer_input + low_back(matmul(attended, output_matrix))
        hidden_two = low(resid_one * rms_scale(resid_one) * feedforward_norm_gain[None, :])
        logits = low_back(matmul(hidden_two, router_matrix))
        gates = jax.nn.softmax(jnp.take_along_axis(logits, expert_choice, axis=1), axis=1)
        shared_pre_gate = low_back(matmul(hidden_two, common_gate_weight))
        shared_pre_up = low_back(matmul(hidden_two, common_up_weight))
        shared_hidden = low(silu_value(shared_pre_gate) * shared_pre_up)
        shared_out = low_back(matmul(shared_hidden, common_down_weight))
        gate_flat = gates.reshape(-1)
        term = jax.checkpoint(partial(routed_term, hidden_two, gate_flat, order_padded, slot_counts, slot_open))

        def slot_adder(carried, slot_items):
            return (carried + term(slot_items), None)
        expert_output_sum, ignored_value = lax.scan(slot_adder, jnp.zeros((TOTAL_TOKENS, MODEL_WIDTH), jnp.float32), (jnp.arange(ROUTED_EXPERTS, dtype=jnp.int32), routed_gate_weight, routed_up_weight, routed_down_weight))
        return resid_one + shared_out + expert_output_sum
    result, pullback = jax.vjp(decoder_layer, tokens.astype(jnp.float32), first_gain.astype(jnp.float32), w_query.astype(jnp.float32), w_key.astype(jnp.float32), w_value.astype(jnp.float32), w_out.astype(jnp.float32), second_gain.astype(jnp.float32), w_router.astype(jnp.float32), shared_gate.astype(jnp.float32), shared_up.astype(jnp.float32), shared_down.astype(jnp.float32), expert_gate.astype(jnp.float32), expert_up.astype(jnp.float32), expert_down.astype(jnp.float32))
    grads = pullback(cotangent.astype(jnp.float32))
    return (result.astype(jnp.bfloat16), grads[0].astype(jnp.bfloat16), grads[1], grads[2], grads[3], grads[4], grads[5], grads[6], grads[7], grads[8], grads[9], grads[10], grads[11], grads[12], grads[13])
```

```python
import math

import jax
import jax.numpy as jnp
from jax import lax
from jax.sharding import PartitionSpec as P

DH = 128
SEQ_MAX = 1024


EPSILON = 1e-06
NEGATIVE = -1e30


def shifted(block, axis, distance):
    devices = range(lax.axis_size(axis))
    route = [(i - distance, i) for i in devices if i - distance in devices]
    return lax.ppermute(block, axis, route)


def shifted_back(block, axis, distance):
    devices = range(lax.axis_size(axis))
    route = [(i, i - distance) for i in devices if i - distance in devices]
    return lax.ppermute(block, axis, route)


def rms_scale(values):
    return lax.rsqrt(jnp.mean(values * values, axis=1, keepdims=True) + EPSILON)


def silu_value(values):
    return values / (1.0 + jnp.exp(-values))


def rotary_tables(position, head_size):
    half_size = head_size // 2
    frequency = 1.0 / 10000.0 ** (jnp.arange(half_size, dtype=jnp.float32) / half_size)
    angles = position.astype(jnp.float32)[:, None] * frequency[None, :]
    cosine_table = jnp.cos(angles)
    sine_table = jnp.sin(angles)
    cosine_table = jnp.concatenate([cosine_table, cosine_table], axis=1)[:, None, :]
    sine_table = jnp.concatenate([sine_table, sine_table], axis=1)[:, None, :]
    return (cosine_table, sine_table)


def rotate(values, cosine_table, sine_table):
    half_size = values.shape[-1] // 2
    turned = jnp.concatenate([-values[..., half_size:], values[..., :half_size]], axis=-1)
    return values * cosine_table + turned * sine_table


def rotate_back(values, cosine_table, sine_table):
    half_size = values.shape[-1] // 2
    scaled = values * sine_table
    turned = jnp.concatenate([scaled[..., half_size:], -scaled[..., :half_size]], axis=-1)
    return values * cosine_table + turned


def norm_back(grad_rows, values, scale_rows, gain_vector):
    weighted = grad_rows * gain_vector[None, :]
    gain_grad = jnp.sum(grad_rows * values * scale_rows, axis=0)
    inner_mean = jnp.mean(weighted * values, axis=1, keepdims=True)
    return (
        scale_rows * weighted - values * (scale_rows * scale_rows * scale_rows) * inner_mean,
        gain_grad,
    )


def sequence_starts(lengths, sequence_order, token_index):
    seq_count = lengths.shape[0]
    picker = sequence_order[:, None] == jnp.arange(seq_count, dtype=jnp.int32)[None, :]
    ordered = jnp.sum(jnp.where(picker, lengths[None, :], 0), axis=1)
    opening = jnp.cumsum(ordered) - ordered
    chosen_open = jnp.where(opening[None, :] <= token_index[:, None], opening[None, :], 0)
    return jnp.max(chosen_open, axis=1)


def project(left, right):
    return jnp.dot(left, right, preferred_element_type=jnp.float32)


def gather(block, axis):
    return lax.all_gather(block, axis, axis=0, tiled=True)


def scatter(block, axis):
    return lax.psum_scatter(block, axis, scatter_dimension=0, tiled=True)


def per_device(
    tokens,
    cotangent,
    lengths,
    sequence_order,
    expert_choice,
    expert_home,
    first_gain,
    w_query,
    w_key,
    w_value,
    w_out,
    second_gain,
    w_router,
    shared_gate,
    shared_up,
    shared_down,
    expert_gate,
    expert_up,
    expert_down,
):
    tok_rows, width = tokens.shape
    experts = expert_home.shape[0]
    local_experts = expert_gate.shape[0]
    hidden = expert_gate.shape[2]
    groups = lax.axis_size("fsdp")
    shard = w_query.shape[0]
    slice_size = shared_down.shape[0]
    att_width = w_query.shape[1]
    heads = att_width // DH
    reach = (SEQ_MAX + tok_rows - 2) // tok_rows
    window = (reach + 1) * tok_rows
    inv_root = 1.0 / math.sqrt(DH)
    place = lax.axis_index("fsdp")
    device = lax.axis_index("rep") * groups + place
    window_parts = [tokens]
    for distance in range(1, reach + 1):
        window_parts.insert(0, shifted(tokens, ("rep", "fsdp"), distance))
    window_tokens = jnp.concatenate(window_parts, axis=0)
    qkv_full = gather(jnp.concatenate([w_query, w_key, w_value], axis=1), "fsdp")
    pad = 128 - experts - 2
    small = jnp.concatenate(
        [
            w_out,
            w_router,
            first_gain[:, None],
            second_gain[:, None],
            jnp.zeros((shard, pad), jnp.bfloat16),
        ],
        axis=1,
    )
    small_full = gather(small, "fsdp")
    out_full = small_full[:, :width]
    router_full = small_full[:, width : width + experts]
    gain_one = small_full[:, width + experts].astype(jnp.float32)
    gain_two = small_full[:, width + experts + 1].astype(jnp.float32)
    shared_pair = jnp.concatenate(
        [
            shared_gate.reshape(shard, groups, slice_size).transpose(1, 0, 2),
            shared_up.reshape(shard, groups, slice_size).transpose(1, 0, 2),
        ],
        axis=2,
    )
    shared_cut = lax.all_to_all(
        shared_pair, "fsdp", split_axis=0, concat_axis=0, tiled=True
    ).reshape(groups * shard, 2 * slice_size)
    cot_all = gather(cotangent, "fsdp")
    choice_all = gather(expert_choice, "fsdp")

    query_index = device * tok_rows + jnp.arange(tok_rows, dtype=jnp.int32)
    key_index = (device - reach) * tok_rows + jnp.arange(window, dtype=jnp.int32)
    start_key = sequence_starts(lengths, sequence_order, key_index)
    start_query = start_key[reach * tok_rows :]
    visible = (
        (key_index[None, :] <= query_index[:, None]) & (key_index[None, :] >= start_query[:, None])
    )[None, :, :]
    cosine_table, sine_table = rotary_tables(key_index - start_key, DH)
    cosine_own = cosine_table[reach * tok_rows :]
    sine_own = sine_table[reach * tok_rows :]

    window_input = window_tokens.astype(jnp.float32)
    normed_window = (window_input * rms_scale(window_input) * gain_one[None, :]).astype(
        jnp.bfloat16
    )
    layer_input = tokens.astype(jnp.float32)
    scale_one = rms_scale(layer_input)
    normed_one = (layer_input * scale_one * gain_one[None, :]).astype(jnp.bfloat16)
    query_raw = project(normed_one, qkv_full[:, :att_width]).reshape(tok_rows, heads, DH)
    key_raw = project(normed_window, qkv_full[:, att_width : 2 * att_width]).reshape(
        window, heads, DH
    )
    value_window = (
        project(normed_window, qkv_full[:, 2 * att_width :])
        .astype(jnp.bfloat16)
        .reshape(window, heads, DH)
    )
    query_rot = rotate(query_raw, cosine_own, sine_own).astype(jnp.bfloat16)
    key_window = rotate(key_raw, cosine_table, sine_table).astype(jnp.bfloat16)
    scores = (
        jnp.einsum("qhd,khd->hqk", query_rot, key_window, preferred_element_type=jnp.float32)
        * inv_root
    )
    masked = jnp.where(visible, scores, NEGATIVE)
    top_score = jnp.max(masked, axis=2, keepdims=True)
    expanded = jnp.exp(masked - top_score)
    denominator = jnp.sum(expanded, axis=2, keepdims=True)
    log_total = top_score + jnp.log(denominator)
    probs_low = (expanded / denominator).astype(jnp.bfloat16)
    mixed_rows = jnp.einsum(
        "hqk,khd->qhd", probs_low, value_window, preferred_element_type=jnp.float32
    )
    attended = mixed_rows.astype(jnp.bfloat16).reshape(tok_rows, att_width)
    resid_one = layer_input + project(attended, out_full)
    scale_two = rms_scale(resid_one)
    normed_two = (resid_one * scale_two * gain_two[None, :]).astype(jnp.bfloat16)
    normed_all = gather(normed_two, "fsdp")

    logits_all = project(normed_all, router_full)
    chosen = jnp.any(
        choice_all[:, :, None] == jnp.arange(experts, dtype=jnp.int32)[None, None, :], axis=1
    )
    gates_all = jax.nn.softmax(jnp.where(chosen, logits_all, NEGATIVE), axis=1)
    slots = place * local_experts + jnp.arange(local_experts, dtype=jnp.int32)
    slot_pick = (expert_home[:, None] == slots[None, :]).astype(jnp.float32)
    gate_slots = jnp.sum(gates_all[:, :, None] * slot_pick[None, :, :], axis=1)

    tail = -(local_experts * hidden + slice_size) % 128
    gate_weight = jnp.concatenate(
        [expert_gate[j] for j in range(local_experts)]
        + [shared_cut[:, :slice_size], jnp.zeros((width, tail), jnp.bfloat16)],
        axis=1,
    )
    up_weight = jnp.concatenate(
        [expert_up[j] for j in range(local_experts)]
        + [shared_cut[:, slice_size:], jnp.zeros((width, tail), jnp.bfloat16)],
        axis=1,
    )
    down_weight = jnp.concatenate(
        [expert_down.reshape(local_experts * hidden, width), shared_down]
        + [jnp.zeros((tail, width), jnp.bfloat16)],
        axis=0,
    )
    down_back = jnp.einsum("td,fd->tf", cot_all, down_weight, preferred_element_type=jnp.float32)
    group_rows = normed_all.shape[0]
    gate_scale = jnp.concatenate(
        [
            jnp.broadcast_to(gate_slots[:, j : j + 1], (group_rows, hidden))
            for j in range(local_experts)
        ]
        + [jnp.ones((group_rows, slice_size + tail), jnp.float32)],
        axis=1,
    )
    pre_gate = project(normed_all, gate_weight)
    pre_up = project(normed_all, up_weight)
    sigmoid = 1.0 / (1.0 + jnp.exp(-pre_gate))
    active = silu_value(pre_gate)
    hidden_rows = (active * pre_up).astype(jnp.bfloat16).astype(jnp.float32)
    gate_grad_slots = jnp.stack(
        [
            jnp.sum(
                hidden_rows[:, j * hidden : (j + 1) * hidden]
                * down_back[:, j * hidden : (j + 1) * hidden],
                axis=1,
            )
            for j in range(local_experts)
        ],
        axis=1,
    )
    hidden_scaled = (hidden_rows * gate_scale).astype(jnp.bfloat16)
    hidden_grad = down_back * gate_scale
    gate_low = (hidden_grad * pre_up * sigmoid * (1.0 + pre_gate * (1.0 - sigmoid))).astype(
        jnp.bfloat16
    )
    up_low = (hidden_grad * active).astype(jnp.bfloat16)
    input_part = jnp.einsum("tf,df->td", gate_low, gate_weight, preferred_element_type=jnp.float32)
    input_part = input_part + jnp.einsum(
        "tf,df->td", up_low, up_weight, preferred_element_type=jnp.float32
    )
    gate_grad_part = jnp.sum(gate_grad_slots[:, None, :] * slot_pick[None, :, :], axis=2)
    gate_grad_high = gate_grad_part.astype(jnp.bfloat16)
    gate_grad_rest = (gate_grad_part - gate_grad_high.astype(jnp.float32)).astype(jnp.bfloat16)
    input_sum = scatter(
        jnp.concatenate(
            [
                input_part.astype(jnp.bfloat16),
                gate_grad_high,
                gate_grad_rest,
                jnp.zeros((group_rows, -2 * experts % 128), jnp.bfloat16),
            ],
            axis=1,
        ),
        "fsdp",
    ).astype(jnp.float32)
    output_part = project(hidden_scaled, down_weight).astype(jnp.bfloat16)
    output_sum = scatter(output_part, "fsdp").astype(jnp.float32)
    output = (resid_one + output_sum).astype(jnp.bfloat16)

    def expert_term(left, right):
        return jnp.einsum("ta,tb->ab", left, right, preferred_element_type=jnp.float32).astype(
            jnp.bfloat16
        )

    down_term = expert_term(hidden_scaled, cot_all)
    expert_down_term = down_term[: local_experts * hidden].reshape(local_experts, hidden, width)
    sdown_term = down_term[local_experts * hidden : local_experts * hidden + slice_size]
    expert_gate_term = jnp.stack(
        [
            expert_term(normed_all, gate_low[:, j * hidden : (j + 1) * hidden])
            for j in range(local_experts)
        ]
    )
    expert_up_term = jnp.stack(
        [
            expert_term(normed_all, up_low[:, j * hidden : (j + 1) * hidden])
            for j in range(local_experts)
        ]
    )
    first_cut = local_experts * hidden
    shared_terms = jnp.concatenate(
        [
            expert_term(normed_all, gate_low[:, first_cut : first_cut + slice_size]),
            expert_term(normed_all, up_low[:, first_cut : first_cut + slice_size]),
        ],
        axis=1,
    )
    shared_back = lax.all_to_all(
        shared_terms.reshape(groups, shard, 2 * slice_size),
        "fsdp",
        split_axis=0,
        concat_axis=0,
        tiled=True,
    )
    sgate_term = shared_back[:, :, :slice_size].transpose(1, 0, 2).reshape(shard, -1)
    sup_term = shared_back[:, :, slice_size:].transpose(1, 0, 2).reshape(shard, -1)

    cotan = cotangent.astype(jnp.float32)
    gates = lax.dynamic_slice_in_dim(gates_all, place * tok_rows, tok_rows, 0)
    gate_grad = (
        input_sum[:, width : width + experts]
        + input_sum[:, width + experts : width + 2 * experts]
    )
    gate_mean = jnp.sum(gates * gate_grad, axis=1, keepdims=True)
    logit_grad = (gates * (gate_grad - gate_mean)).astype(jnp.bfloat16)
    router_term = jnp.einsum(
        "td,te->de", normed_two, logit_grad, preferred_element_type=jnp.float32
    )
    normed_two_grad = input_sum[:, :width] + jnp.einsum(
        "te,de->td", logit_grad, router_full, preferred_element_type=jnp.float32
    )
    resid_part, gain_two_term = norm_back(normed_two_grad, resid_one, scale_two, gain_two)
    resid_grad = cotan + resid_part
    out_grad_low = resid_grad.astype(jnp.bfloat16)
    out_term = jnp.einsum("ta,td->ad", attended, out_grad_low, preferred_element_type=jnp.float32)
    attended_grad = (
        jnp.einsum("td,ad->ta", out_grad_low, out_full, preferred_element_type=jnp.float32)
        .astype(jnp.bfloat16)
        .reshape(tok_rows, heads, DH)
    )
    scores_back = (
        jnp.einsum("qhd,khd->hqk", query_rot, key_window, preferred_element_type=jnp.float32)
        * inv_root
    )
    probs_back = jnp.exp(jnp.where(visible, scores_back, NEGATIVE) - log_total)
    probs_back_low = probs_back.astype(jnp.bfloat16)
    probs_grad = jnp.einsum(
        "qhd,khd->hqk", attended_grad, value_window, preferred_element_type=jnp.float32
    )
    inner_sum = jnp.sum(probs_back * probs_grad, axis=2, keepdims=True)
    scores_grad = (probs_back * (probs_grad - inner_sum)).astype(jnp.bfloat16)
    query_grad_rot = (
        jnp.einsum("hqk,khd->qhd", scores_grad, key_window, preferred_element_type=jnp.float32)
        * inv_root
    )
    key_grad_rot = (
        jnp.einsum("hqk,qhd->khd", scores_grad, query_rot, preferred_element_type=jnp.float32)
        * inv_root
    )
    value_grad = (
        jnp.einsum("hqk,qhd->khd", probs_back_low, attended_grad, preferred_element_type=jnp.float32)
        .astype(jnp.bfloat16)
        .reshape(window, att_width)
    )
    query_grad = (
        rotate_back(query_grad_rot, cosine_own, sine_own)
        .astype(jnp.bfloat16)
        .reshape(tok_rows, att_width)
    )
    key_grad = (
        rotate_back(key_grad_rot, cosine_table, sine_table)
        .astype(jnp.bfloat16)
        .reshape(window, att_width)
    )
    key_value_back = jnp.einsum(
        "ta,da->td",
        jnp.concatenate([key_grad, value_grad], axis=1),
        qkv_full[:, att_width:],
        preferred_element_type=jnp.float32,
    )
    normed_one_grad = key_value_back[reach * tok_rows :] + jnp.einsum(
        "ta,da->td", query_grad, qkv_full[:, :att_width], preferred_element_type=jnp.float32
    )
    for distance in range(1, reach + 1):
        lower = (reach - distance) * tok_rows
        normed_one_grad = normed_one_grad + shifted_back(
            key_value_back[lower : lower + tok_rows].astype(jnp.bfloat16),
            ("rep", "fsdp"),
            distance,
        ).astype(jnp.float32)
    query_term = jnp.einsum("td,ta->da", normed_one, query_grad, preferred_element_type=jnp.float32)
    key_term = jnp.einsum(
        "td,ta->da", normed_window, key_grad, preferred_element_type=jnp.float32
    )
    value_term = jnp.einsum(
        "td,ta->da", normed_window, value_grad, preferred_element_type=jnp.float32
    )
    input_back, gain_one_term = norm_back(normed_one_grad, layer_input, scale_one, gain_one)
    input_grad = (resid_grad + input_back).astype(jnp.bfloat16)
    dense_share = scatter(
        jnp.concatenate(
            [
                out_term.astype(jnp.bfloat16),
                query_term.astype(jnp.bfloat16),
                key_term.astype(jnp.bfloat16),
                value_term.astype(jnp.bfloat16),
            ],
            axis=1,
        ),
        "fsdp",
    )
    small_share = scatter(
        jnp.concatenate(
            [
                router_term.astype(jnp.bfloat16),
                gain_one_term.astype(jnp.bfloat16)[:, None],
                gain_two_term.astype(jnp.bfloat16)[:, None],
                jnp.zeros((width, pad), jnp.bfloat16),
            ],
            axis=1,
        ),
        "fsdp",
    )
    summed = lax.psum(
        (
            expert_gate_term,
            expert_up_term,
            expert_down_term,
            sgate_term,
            sup_term,
            sdown_term,
            dense_share,
            small_share,
        ),
        "rep",
    )
    (
        expert_gate_sum,
        expert_up_sum,
        expert_down_sum,
        sgate_sum,
        sup_sum,
        sdown_sum,
        dense_sum,
        small_sum,
    ) = [value.astype(jnp.float32) for value in summed]
    return (
        output,
        input_grad,
        small_sum[:, experts],
        dense_sum[:, width : width + att_width],
        dense_sum[:, width + att_width : width + 2 * att_width],
        dense_sum[:, width + 2 * att_width :],
        dense_sum[:, :width],
        small_sum[:, experts + 1],
        small_sum[:, :experts],
        sgate_sum,
        sup_sum,
        sdown_sum,
        expert_gate_sum,
        expert_up_sum,
        expert_down_sum,
    )


def solution(mesh):
    placed = (
        P(("rep", "fsdp"), None),
        P(("rep", "fsdp"), None),
        P(),
        P(),
        P(("rep", "fsdp"), None),
        P(),
        P("fsdp"),
        P("fsdp", None),
        P("fsdp", None),
        P("fsdp", None),
        P("fsdp", None),
        P("fsdp"),
        P("fsdp", None),
        P("fsdp", None),
        P("fsdp", None),
        P("fsdp", None),
        P("fsdp", None, None),
        P("fsdp", None, None),
        P("fsdp", None, None),
    )
    return jax.shard_map(
        per_device,
        mesh=mesh,
        in_specs=placed,
        out_specs=(
            P(("rep", "fsdp"), None),
            P(("rep", "fsdp"), None),
            P("fsdp"),
            P("fsdp", None),
            P("fsdp", None),
            P("fsdp", None),
            P("fsdp", None),
            P("fsdp"),
            P("fsdp", None),
            P("fsdp", None),
            P("fsdp", None),
            P("fsdp", None),
            P("fsdp", None, None),
            P("fsdp", None, None),
            P("fsdp", None, None),
        ),
        check_vma=False,
    )
```
